128 devices in a mesh: dp: 8 (over z, core), tensor: 16 (over y, x).
Axes of the slice: x: 4, y: 4, z: 4, core: 2. Of those that a mesh axis runs over, the one named last changes fastest.
Arguments:
- inputs: bfloat16 [8192, 8192], P('dp', 'tensor'), may hold values from -6 to 6
- output_gradient: bfloat16 [8192, 8192], P('dp', 'tensor'), may hold values from -6 to 6
- weight: bfloat16 [8192, 8192], P(None, 'tensor'), may hold values from -0.0625 to 0.0625
- adapter_down_factor: bfloat16 [1024, 16, 8192], P('dp', None, 'tensor'), may hold values from -0.0625 to 0.0625
- adapter_up_factor: bfloat16 [1024, 16, 8192], P('dp', None, 'tensor'), may hold values from -0.0625 to 0.0625
- block_adapter_index: int32 [64], P('dp'), may hold values from 0 to 1023
- adapter_table_slot: int32 [1024], replicated, may hold values from 0 to 1023, each once
Outputs:
- input_gradient: bfloat16 [8192, 8192], P('dp', 'tensor')
- grad_down: float32 [1024, 16, 8192], P('dp', None, 'tensor')
- grad_up: float32 [1024, 16, 8192], P('dp', None, 'tensor')
The draws below stay inside these ranges and needn't reach their ends.
Inputs may be any that keep to these rules, and one draw needn't show every extreme that they name: `adapter_table_slot`: each slot is used by exactly one adapter.
All inputs are finite; a program needn't handle non-finite values.
Results may differ from the reference program's by a relative error of at most 0.003.
Values may be sent and summed in bfloat16 or wider, within the bound.
No kernel may reach another device: no remote copies, remote signals or barrier semaphores. Data moves between devices by JAX's collectives and lax.ppermute only.
A program may use at most 192 MiB of HBM per device.

```python
import math
import jax
import jax.numpy as jnp
import numpy as np

MODEL_WIDTH = 8192
ADAPTER_RANK = 16
BLOCK = 128
ADAPTER_TOTAL = 1024
TOKEN_ROWS = 8192
BLOCKS = 64


def place_ends(drawn, key, least, high):
    spot = [jax.random.randint(jax.random.fold_in(key, axis), (), 0, length) for axis, length in enumerate(drawn.shape)]
    main_axis = drawn.shape.index(max(drawn.shape))
    neighbour = spot[:main_axis] + [(spot[main_axis] + 1) % drawn.shape[main_axis]] + spot[main_axis + 1:]
    return drawn.at[tuple(spot)].set(least).at[tuple(neighbour)].set(high)


def block_levels(stream_key, shape, split, low, high):
    def one(position, parts):
        steps = jax.random.uniform(jax.random.fold_in(jax.random.fold_in(stream_key, 6), position), (parts,), jnp.float32, low / len(split), high / len(split))
        return jnp.repeat(jnp.exp(steps), shape[position] // parts).reshape((-1,) + (1,) * (len(shape) - position - 1))

    level = one(*split[0])
    for cut in split[1:]:
        level = level * one(*cut)
    return level


def rank_bounds(amount, skew):
    loads = [(1 << 20) // math.isqrt(standing ** skew) + 1 for standing in range(1, amount + 1)]
    scale = 1 + sum(loads) // (1 << 30)
    return np.cumsum(np.array([max(1, weight // scale) for weight in loads]))


def ranked(stream_key, extent, count, slope):
    table = rank_bounds(count, slope)
    ticket = jax.random.randint(jax.random.fold_in(stream_key, 1), extent, 0, int(table[count - 1]))
    standing = jnp.searchsorted(jnp.asarray(table, jnp.int32), ticket, side="right")
    return jax.random.permutation(jax.random.fold_in(stream_key, 2), count)[standing].astype(jnp.int32)


def scatter_about(rng, dims, deviation, most, cuts=(), held_as=jnp.bfloat16):
    result = deviation * jax.random.normal(rng, dims, jnp.float32)
    if cuts:
        result = result * block_levels(rng, dims, cuts, -0.22, 0.18)
    return jnp.clip(result, -most, most).astype(held_as)


def setup_inputs(seed: int = 0) -> dict:
    arg_keys = jax.random.split(jax.random.key(seed), 8)
    inputs = scatter_about(arg_keys[0], (TOKEN_ROWS, MODEL_WIDTH), 1.0, 6.0, ((0, 8), (1, 16)))
    output_gradient = scatter_about(arg_keys[1], (TOKEN_ROWS, MODEL_WIDTH), 1.0, 6.0, ((0, 8), (1, 16)))
    weight = scatter_about(arg_keys[2], (MODEL_WIDTH, MODEL_WIDTH), MODEL_WIDTH ** -0.5, 0.0625, ((1, 16),))
    adapter_down_factor = scatter_about(arg_keys[3], (ADAPTER_TOTAL, ADAPTER_RANK, MODEL_WIDTH), MODEL_WIDTH ** -0.5, 0.0625, ((0, 8), (2, 16)))
    adapter_up_factor = scatter_about(arg_keys[4], (ADAPTER_TOTAL, ADAPTER_RANK, MODEL_WIDTH), MODEL_WIDTH ** -0.5, 0.0625, ((0, 8), (2, 16)))
    block_adapter_index = place_ends(ranked(arg_keys[5], (BLOCKS,), ADAPTER_TOTAL, 2), jax.random.fold_in(arg_keys[5], 3), 0, ADAPTER_TOTAL - 1).astype(jnp.int32)
    adapter_table_slot = jax.random.permutation(arg_keys[6], ADAPTER_TOTAL).astype(jnp.int32)
    return dict(inputs=inputs, output_gradient=output_gradient, weight=weight, adapter_down_factor=adapter_down_factor, adapter_up_factor=adapter_up_factor, block_adapter_index=block_adapter_index, adapter_table_slot=adapter_table_slot)


adapter_scale = 2.0


def reference(inputs, output_gradient, weight, adapter_down_factor, adapter_up_factor, block_adapter_index, adapter_table_slot):
    slot_index_list = adapter_table_slot[block_adapter_index].astype(jnp.int32)
    down_factor_blocks = adapter_down_factor[slot_index_list].astype(jnp.float32)
    up_factor_blocks = adapter_up_factor[slot_index_list].astype(jnp.float32)
    input_blocks = inputs.reshape(BLOCKS, BLOCK, MODEL_WIDTH).astype(jnp.float32)
    output_gradient_blocks = output_gradient.reshape(BLOCKS, BLOCK, MODEL_WIDTH).astype(jnp.float32)
    hidden_activation = jnp.einsum("nvh,nwh->nvw", input_blocks, down_factor_blocks)
    projected_gradient = jnp.einsum("nvh,nwh->nvw", output_gradient_blocks, up_factor_blocks)
    hidden_lowrank = hidden_activation.astype(jnp.bfloat16).astype(jnp.float32)
    projected_gradient_lowrank = projected_gradient.astype(jnp.bfloat16).astype(jnp.float32)
    frozen_input_gradient = jnp.dot(output_gradient, weight.T, preferred_element_type=jnp.float32)
    adapter_input_gradient = jnp.einsum("wmx,wxv->wmv", projected_gradient_lowrank, down_factor_blocks).reshape(TOKEN_ROWS, MODEL_WIDTH)
    input_gradient = (frozen_input_gradient + adapter_scale * adapter_input_gradient).astype(jnp.bfloat16)
    block_down_factor = adapter_scale * jnp.einsum("eyw,eyi->ewi", projected_gradient_lowrank, input_blocks)
    block_up_factor = adapter_scale * jnp.einsum("eyw,eyi->ewi", hidden_lowrank, output_gradient_blocks)
    grad_down = jnp.zeros((ADAPTER_TOTAL, ADAPTER_RANK, MODEL_WIDTH), jnp.float32).at[slot_index_list].add(block_down_factor)
    grad_up = jnp.zeros((ADAPTER_TOTAL, ADAPTER_RANK, MODEL_WIDTH), jnp.float32).at[slot_index_list].add(block_up_factor)
    return input_gradient, grad_down, grad_up
```

```python
import jax
import jax.numpy as jnp
from jax import lax
from jax.experimental import pallas as pl
from jax.experimental.pallas import tpu as pltpu
from jax.sharding import PartitionSpec as P


BLOCK = 128
ADAPTER_SCALE = 2.0
SIDE = 4
CORES = 2
CORE, DP = 8, 9
SMEM = pl.BlockSpec(memory_space=pltpu.SMEM)
ANY = pl.BlockSpec(memory_space=pl.ANY)


def from_x(a, k):
    return lax.ppermute(
        a, "tensor", [(SIDE * y + (x + k) % SIDE, SIDE * y + x) for y in range(SIDE) for x in range(SIDE)]
    )


def from_y(a, k):
    return lax.ppermute(
        a, "tensor", [(SIDE * ((y + k) % SIDE) + x, SIDE * y + x) for y in range(SIDE) for x in range(SIDE)]
    )


def from_z(a, k):
    return lax.ppermute(
        a, "dp", [(CORES * ((z + k) % SIDE) + c, CORES * z + c) for z in range(SIDE) for c in range(CORES)]
    )


def from_partner(a):
    return lax.ppermute(
        a, "dp", [(CORES * z + 1 - c, CORES * z + c) for z in range(SIDE) for c in range(CORES)]
    )


def dot_nt(a, b):
    return lax.dot_general(a, b, (((1,), (1,)), ((), ())), preferred_element_type=jnp.float32)


def cost(flops, nbytes):
    return pl.CostEstimate(flops=flops, bytes_accessed=nbytes, transcendentals=0)


def pick_factors(slots, place, down, up, kz, nb):
    owned, rank, width = down.shape

    def body(slots_ref, place_ref, down_ref, up_ref, same_ref, other_ref, sem):
        def each(step):
            for r, out in enumerate((same_ref, other_ref)):
                for k in range(kz):
                    for b in range(nb):
                        at = (k * CORES + r) * nb + b
                        step(slots_ref[at] - place_ref[DP] * owned, out, k, b, at)

        def copies(slot, out, k, b, at):
            return (
                pltpu.make_async_copy(down_ref.at[slot], out.at[k, b, 0], sem.at[at, 0]),
                pltpu.make_async_copy(up_ref.at[slot], out.at[k, b, 1], sem.at[at, 1]),
            )

        def begin(slot, out, k, b, at):
            mine = (slot >= 0) & (slot < owned)

            @pl.when(mine)
            def _():
                for cp in copies(slot, out, k, b, at):
                    cp.start()

            @pl.when(jnp.logical_not(mine))
            def _():
                out[k, b] = jnp.zeros((2, rank, width), out.dtype)

        def end(slot, out, k, b, at):
            @pl.when((slot >= 0) & (slot < owned))
            def _():
                for cp in copies(slot, out, k, b, at):
                    cp.wait()

        each(begin)
        each(end)

    shape = jax.ShapeDtypeStruct((kz, nb, 2, rank, width), down.dtype)
    vmem = pl.BlockSpec(memory_space=pltpu.VMEM)
    return pl.pallas_call(
        body,
        out_shape=(shape, shape),
        in_specs=[SMEM, SMEM, ANY, ANY],
        out_specs=(vmem, vmem),
        scratch_shapes=[pltpu.SemaphoreType.DMA((kz * CORES * nb, 2))],
        name="pick_factors",
        cost_estimate=cost(0, 4 * 2**20),
    )(slots, place, down, up)


def rank_partials(parts, inputs, grads):
    nb, _, rank, width = parts[0].shape
    each = nb // 2

    def body(p0, p1, p2, p3, in_ref, og_ref, f_ref, r_ref):
        f32 = jnp.float32
        for b in range(each):
            f = p0[b].astype(f32) + p1[b].astype(f32) + p2[b].astype(f32) + p3[b].astype(f32)
            f = f.astype(f_ref.dtype)
            f_ref[b] = f
            rows = pl.ds(b * BLOCK, BLOCK)
            r_ref[b, :rank] = dot_nt(f[0], in_ref[rows, :])
            r_ref[b, rank:] = dot_nt(f[1], og_ref[rows, :])

    factor = pl.BlockSpec((each, 2, rank, width), lambda i: (i, 0, 0, 0))
    rows = pl.BlockSpec((each * BLOCK, width), lambda i: (i, 0))
    return pl.pallas_call(
        body,
        grid=(2,),
        out_shape=(
            jax.ShapeDtypeStruct(parts[0].shape, parts[0].dtype),
            jax.ShapeDtypeStruct((nb, 2 * rank, BLOCK), jnp.float32),
        ),
        in_specs=[factor] * 4 + [rows, rows],
        out_specs=(factor, pl.BlockSpec((each, 2 * rank, BLOCK), lambda i: (i, 0, 0))),
        name="rank_partials",
        cost_estimate=cost(2 * nb * 2 * rank * BLOCK * width, 8 * 2**20),
    )(*parts, inputs, grads)


def block_gradients(sums, inputs, grads):
    nb, rank2, _ = sums.shape
    rank, width = rank2 // 2, inputs.shape[1]
    each = nb // 2

    def body(s_ref, in_ref, og_ref, g_ref):
        for b in range(each):
            low = s_ref[b].astype(jnp.bfloat16)
            rows = pl.ds(b * BLOCK, BLOCK)
            down = jnp.dot(low[rank:], in_ref[rows, :], preferred_element_type=jnp.float32)
            up = jnp.dot(low[:rank], og_ref[rows, :], preferred_element_type=jnp.float32)
            g_ref[b, 0] = (ADAPTER_SCALE * down).astype(g_ref.dtype)
            g_ref[b, 1] = (ADAPTER_SCALE * up).astype(g_ref.dtype)

    rows = pl.BlockSpec((each * BLOCK, width), lambda i: (i, 0))
    return pl.pallas_call(
        body,
        grid=(2,),
        out_shape=jax.ShapeDtypeStruct((nb, 2, rank, width), jnp.bfloat16),
        in_specs=[pl.BlockSpec((each, rank2, BLOCK), lambda i: (i, 0, 0)), rows, rows],
        out_specs=pl.BlockSpec((each, 2, rank, width), lambda i: (i, 0, 0, 0)),
        name="block_gradients",
        cost_estimate=cost(2 * nb * rank2 * BLOCK * width, 6 * 2**20),
    )(sums, inputs, grads)


def sum_by_slot(slots, place, same, other, owned):
    kz, nb, _, rank, width = other.shape
    group = min(64, owned)

    def body(slots_ref, place_ref, g0, g1, g2, g3, o_ref, gd_ref, gu_ref):
        base = place_ref[DP] * owned + pl.program_id(0) * group
        gd_ref[...] = jnp.zeros_like(gd_ref)
        gu_ref[...] = jnp.zeros_like(gu_ref)
        for k, g in enumerate((g0, g1, g2, g3)):
            for r in range(CORES):

                def one(b, carry, k=k, g=g, r=r):
                    at = slots_ref[(k * CORES + r) * nb + b] - base

                    @pl.when((at >= 0) & (at < group))
                    def _():
                        block = (o_ref[k, b] if r else g[b]).astype(jnp.float32)
                        gd_ref[at] = gd_ref[at] + block[0]
                        gu_ref[at] = gu_ref[at] + block[1]

                    return carry

                lax.fori_loop(0, nb, one, 0)

    piece = pl.BlockSpec((nb, 2, rank, width), lambda i: (0, 0, 0, 0))
    out = pl.BlockSpec((group, rank, width), lambda i: (i, 0, 0))
    shape = jax.ShapeDtypeStruct((owned, rank, width), jnp.float32)
    return pl.pallas_call(
        body,
        grid=(owned // group,),
        out_shape=(shape, shape),
        in_specs=[SMEM, SMEM] + [piece] * kz + [pl.BlockSpec(other.shape, lambda i: (0, 0, 0, 0, 0))],
        out_specs=(out, out),
        name="sum_by_slot",
        cost_estimate=cost(2**20, 20 * 2**20),
    )(slots, place, *same, other)


def base_product(s, place, og, og_far, weight, near, far, adapter=None):
    rows, width = og.shape
    half = near[0].shape[1]
    n, depth = 2 * half, SIDE * width
    tile = 2 * BLOCK
    steps = rows // tile
    out_type = jnp.float32 if adapter else jnp.bfloat16

    def body(place_ref, o0, o1, o2, o3, w_ref, *refs):
        pieces = (refs[:SIDE], refs[SIDE : 2 * SIDE])
        extra = refs[2 * SIDE : -7]
        out_ref, o_all, w_all, out_all, o_sem, w_sem, out_sem = refs[-7:]
        core = place_ref[CORE]
        row = pl.multiple_of(place_ref[s] * n, n)
        own = pltpu.make_async_copy(w_ref.at[pl.ds(row, n), :], w_all.at[:, pl.ds(0, width)], w_sem.at[0])

        def each_piece(step):
            for d in range(SIDE):

                @pl.when(place_ref[SIDE + s] == d)
                def _():
                    for side in range(2):
                        at = pl.multiple_of((core if side == 0 else 1 - core) * half, half)
                        for k in range(1, SIDE):
                            step(
                                pltpu.make_async_copy(
                                    pieces[side][d].at[k - 1],
                                    w_all.at[pl.ds(at, half), pl.ds(k * width, width)],
                                    w_sem.at[side * SIDE + k],
                                )
                            )

        def each_tile(t, step):
            for k, o in enumerate((o0, o1, o2, o3)):
                r = pl.ds(t * tile, tile)
                step(pltpu.make_async_copy(o.at[r, :], o_all.at[r, pl.ds(k * width, width)], o_sem.at[t, k]))

        def leave(t):
            r = pl.ds(t * tile, tile)
            return pltpu.make_async_copy(out_all.at[r, :], out_ref.at[r, :], out_sem.at[t])

        own.start()
        each_piece(lambda cp: cp.start())
        for t in range(steps):
            each_tile(t, lambda cp: cp.start())
        own.wait()
        each_piece(lambda cp: cp.wait())
        for t in range(steps):
            each_tile(t, lambda cp: cp.wait())
            r = pl.ds(t * tile, tile)
            acc = dot_nt(o_all[r, :], w_all[...])
            if adapter:
                sums_ref, f_ref = extra
                terms = []
                for b in range(t * tile // BLOCK, (t + 1) * tile // BLOCK):
                    g = sums_ref[b, f_ref.shape[2] :].astype(jnp.bfloat16)
                    terms.append(
                        lax.dot_general(
                            g, f_ref[b, 0], (((0,), (0,)), ((), ())), preferred_element_type=jnp.float32
                        )
                    )
                acc = acc + ADAPTER_SCALE * jnp.concatenate(terms, axis=0)
            out_all[r, :] = acc.astype(out_type)
            leave(t).start()
        for t in range(steps):
            leave(t).wait()

    return pl.pallas_call(
        body,
        out_shape=jax.ShapeDtypeStruct((rows, n), out_type),
        in_specs=[SMEM] + [ANY] * 13 + ([pl.BlockSpec(memory_space=pltpu.VMEM)] * 2 if adapter else []),
        out_specs=ANY,
        scratch_shapes=[
            pltpu.VMEM((rows, depth), og.dtype),
            pltpu.VMEM((n, depth), og.dtype),
            pltpu.VMEM((rows, n), out_type),
            pltpu.SemaphoreType.DMA((steps, SIDE)),
            pltpu.SemaphoreType.DMA((2 * SIDE,)),
            pltpu.SemaphoreType.DMA((steps,)),
        ],
        cost_estimate=cost(2 * rows * depth * n, 16 * 2**20),
    )(place, og, *og_far, weight, *near, *far, *(adapter or ()))


def per_device(
    inputs,
    output_gradient,
    weight,
    adapter_down_factor,
    adapter_up_factor,
    block_adapter_index,
    adapter_table_slot,
):
    row_count, width = inputs.shape
    nb = row_count // BLOCK
    owned = adapter_down_factor.shape[0]
    half = width // CORES
    dp_id = lax.axis_index("dp")
    t_id = lax.axis_index("tensor")
    z, c = dp_id // CORES, dp_id % CORES
    y, x = t_id // SIDE, t_id % SIDE

    i = lax.iota(jnp.int32, 16)
    place = jnp.where(i < SIDE, SIDE * ((y + i) % SIDE) + x, (y + i - z) % SIDE)
    place = jnp.where(i == CORE, c, jnp.where(i == DP, dp_id, place)).astype(jnp.int32)

    table_ids = lax.broadcasted_iota(jnp.int32, (nb, adapter_table_slot.shape[0]), 1)
    my_slots = jnp.sum(
        jnp.where(block_adapter_index[:, None] == table_ids, adapter_table_slot[None, :], 0), axis=1
    )
    pair = jnp.concatenate([my_slots, from_partner(my_slots)])
    slots = jnp.concatenate([pair] + [from_z(pair, k) for k in range(1, SIDE)])

    sent = []
    for k in range(1, SIDE):
        row = (SIDE * z + (x - k) % SIDE) * width + c * half
        sent.append(from_x(lax.dynamic_slice_in_dim(weight, row, half, 0), k))
    near = [jnp.stack(sent)]
    near += [from_z(near[0], k) for k in range(1, SIDE)]
    far = [from_partner(p) for p in near]

    og_far = [from_x(output_gradient, k) for k in range(1, SIDE)]

    same, other = pick_factors(slots, place, adapter_down_factor, adapter_up_factor, SIDE, nb)
    merged = same + from_partner(other)
    parts = [merged[0]] + [from_z(merged[k], -k) for k in range(1, SIDE)]
    factors, sums = rank_partials(parts, inputs, output_gradient)
    sums = sums + from_y(sums, 1)
    sums = sums + from_y(sums, 2)
    sums = sums + from_x(sums, 1)
    sums = sums + from_x(sums, 2)

    block_grads = block_gradients(sums, inputs, output_gradient)
    same_grads = [block_grads] + [from_z(block_grads, k) for k in range(1, SIDE)]
    other_grads = from_partner(jnp.stack(same_grads))
    grad_down, grad_up = sum_by_slot(slots, place, same_grads, other_grads, owned)

    arrived = []
    for s in (2, 1, 3):
        part = base_product(s, place, output_gradient, og_far, weight, near, far)
        arrived.append(from_y(part, -s))
    total = base_product(0, place, output_gradient, og_far, weight, near, far, (sums, factors))
    for part in arrived:
        total = total + part.astype(jnp.float32)
    input_gradient = total.astype(jnp.bfloat16)
    return input_gradient, grad_down, grad_up


def solution(mesh):
    return jax.shard_map(
        per_device,
        mesh=mesh,
        in_specs=(
            P("dp", "tensor"),
            P("dp", "tensor"),
            P(None, "tensor"),
            P("dp", None, "tensor"),
            P("dp", None, "tensor"),
            P("dp"),
            P(),
        ),
        out_specs=(P("dp", "tensor"), P("dp", None, "tensor"), P("dp", None, "tensor")),
        check_vma=False,
    )
```
